32 devices in a mesh: dp: 16 (over z, y, x), fsdp: 2 (over core).
Axes of the slice: x: 2, y: 2, z: 4, core: 2. Of those that a mesh axis runs over, the one named last changes fastest.
Arguments:
- tokens: bfloat16 [4096, 2048], P(('dp', 'fsdp')), may hold values from -6 to 6
- cotangent: bfloat16 [4096, 2048], P(('dp', 'fsdp')), may hold values from -6 to 6
- group_size: int32 [32], P(('dp', 'fsdp')), may hold values from 4 to 16, as said below
- prefix_len: int32 [32], P(('dp', 'fsdp')), may hold values from 16 to 32, as said below
- sol_len: int32 [32, 16], P(('dp', 'fsdp')), may hold values from 0 to 109, as said below
- ln1_gain: bfloat16 [2048], P(('dp', 'fsdp')), may hold values from 0.099609375 to 1.8984375
- ln1_bias: bfloat16 [2048], P(('dp', 'fsdp')), may hold values from -3 to 3
- w_qkv: bfloat16 [2048, 6144], P(('dp', 'fsdp')), may hold values from -0.125 to 0.125
- q_bias: bfloat16 [2048], P(('dp', 'fsdp')), may hold values from -3 to 3
- v_bias: bfloat16 [2048], P(('dp', 'fsdp')), may hold values from -3 to 3
- w_out: bfloat16 [2048, 2048], P(('dp', 'fsdp')), may hold values from -1 to 1
- out_bias: bfloat16 [2048], P(('dp', 'fsdp')), may hold values from -3 to 3
- ln2_gain: bfloat16 [2048], P(('dp', 'fsdp')), may hold values from 0.099609375 to 1.8984375
- ln2_bias: bfloat16 [2048], P(('dp', 'fsdp')), may hold values from -3 to 3
- w_up: bfloat16 [2048, 8192], P(('dp', 'fsdp')), may hold values from -0.125 to 0.125
- up_bias: bfloat16 [8192], P(('dp', 'fsdp')), may hold values from -3 to 3
- w_down: bfloat16 [8192, 2048], P(('dp', 'fsdp')), may hold values from -0.0625 to 0.0625
- down_bias: bfloat16 [2048], P(('dp', 'fsdp')), may hold values from -3 to 3
Outputs:
- layer_out: bfloat16 [4096, 2048], P(('dp', 'fsdp'))
- tokens_grad: bfloat16 [4096, 2048], P(('dp', 'fsdp'))
- ln1_gain_grad: float32 [2048], P(('dp', 'fsdp'))
- ln1_bias_grad: float32 [2048], P(('dp', 'fsdp'))
- w_qkv_grad: float32 [2048, 6144], P(('dp', 'fsdp'))
- q_bias_grad: float32 [2048], P(('dp', 'fsdp'))
- v_bias_grad: float32 [2048], P(('dp', 'fsdp'))
- w_out_grad: float32 [2048, 2048], P(('dp', 'fsdp'))
- out_bias_grad: float32 [2048], P(('dp', 'fsdp'))
- ln2_gain_grad: float32 [2048], P(('dp', 'fsdp'))
- ln2_bias_grad: float32 [2048], P(('dp', 'fsdp'))
- w_up_grad: float32 [2048, 8192], P(('dp', 'fsdp'))
- up_bias_grad: float32 [8192], P(('dp', 'fsdp'))
- w_down_grad: float32 [8192, 2048], P(('dp', 'fsdp'))
- down_bias_grad: float32 [2048], P(('dp', 'fsdp'))
The draws below stay inside these ranges and needn't reach their ends.
Inputs may be any that keep to these rules, and one draw needn't show every extreme that they name: `group_size`: some group has 16 solutions and some group 4. `prefix_len`: some group has a prefix of 128 // 8 tokens and some one of 128 // 4. `sol_len`: entries from group_size[g] on are 0, the others 1 or more; a group's prefix and solutions together take at most 128 slots, exactly 128 in some group, and half of them or more in every group; some solution reaches the most.
All inputs are finite; a program needn't handle non-finite values.
Results may differ from the reference program's by a relative error of at most 0.012.
Values may be sent and summed in bfloat16 or wider, within the bound.
A program may use at most 384 MiB of HBM per device.

```python
import jax
import jax.numpy as jnp
from jax import lax

D = 2048
HEADS = 16
FF = 8192
TOK_DEV = 128
MAX_SOL = 16
GROUPS = 32
TOKENS = 4096


def layout(key):
    groups = GROUPS
    slots = TOK_DEV
    most = MAX_SOL
    base = jax.random.fold_in(key, 31)
    key_count, key_prefix, key_spare, key_weight = jax.random.split(base, 4)
    group_index = jnp.arange(groups, dtype=jnp.int32)
    counts = jax.random.randint(key_count, (groups,), 4, most + 1, dtype=jnp.int32)
    counts = jnp.where(group_index == 0, most, jnp.where((group_index == 1) | (group_index == 2), 4, counts))
    prefix_low = slots // 8
    prefix_high = slots // 4
    prefixes = jax.random.randint(key_prefix, (groups,), prefix_low, prefix_high + 1, dtype=jnp.int32)
    prefixes = jnp.where(group_index == 1, prefix_high, jnp.where(group_index == 2, prefix_low, prefixes))
    spares = jax.random.randint(key_spare, (groups,), 0, slots // 2 + 1, dtype=jnp.int32)
    spares = jnp.where((group_index == 0) | (group_index == 2), 0, spares)
    spans = slots - spares - prefixes
    slot_index = jnp.arange(most, dtype=jnp.int32)
    living = (slot_index[None, :] < counts[:, None]).astype(jnp.int32)
    shares = jax.random.randint(key_weight, (groups, most), 1, 6, dtype=jnp.int32) * living
    first_only = (slot_index[None, :] == 0).astype(jnp.int32)
    shares = jnp.where((group_index == 2)[:, None], first_only, shares)
    portion = shares * (spans - counts)[:, None] // jnp.sum(shares, axis=1, keepdims=True)
    lengths = living + portion
    remains = spans - jnp.sum(lengths, axis=1)
    lengths = lengths + (slot_index[None, :] == 0).astype(jnp.int32) * remains[:, None]
    return (counts.astype(jnp.int32), prefixes.astype(jnp.int32), lengths.astype(jnp.int32))


def draw_group_size(key, part):
    return layout(key)[0]


def draw_prefix_len(key, part):
    return layout(key)[1]


def draw_sol_len(key, part):
    return layout(key)[2]


def with_spikes(array, stream_key, source, target, shards_of, factor):
    owner, partner = [(jnp.arange(array.shape[position]) // (array.shape[position] // shards_of)).reshape([-1 if axis == position else 1 for axis in range(array.ndim)]) for position in (source, target)]
    chosen = jax.random.permutation(stream_key, shards_of)[partner]
    strong = (owner == chosen) | (owner == (partner + shards_of // 2) % shards_of)
    return jnp.where(strong, factor * array, array)


def levels(stream_key, extent, pieces, least, top_value):
    level = 1.0
    for axis_at, shards_of in pieces:
        heights = jax.random.uniform(jax.random.fold_in(jax.random.fold_in(stream_key, 6), axis_at), (shards_of,), jnp.float32, least / len(pieces), top_value / len(pieces))
        level = level * jnp.repeat(jnp.exp(heights), extent[axis_at] // shards_of).reshape((-1,) + (1,) * (len(extent) - 1 - axis_at))
    return level


def gaussian(key, dims, scale, most, shards=(), kind=jnp.bfloat16):
    result = scale * jax.random.normal(key, dims, jnp.float32)
    if shards:
        result = result * levels(key, dims, shards, -0.22, 0.18)
    return jnp.clip(result, -most, most).astype(kind)


def noise_with(own_key, dims, deviation, most, pieces, heavy, kind=jnp.bfloat16):
    entries = deviation * jax.random.normal(own_key, dims, jnp.float32)
    if pieces:
        entries = entries * levels(own_key, dims, pieces, -0.22, 0.18)
    return jnp.clip(with_spikes(entries, jax.random.fold_in(own_key, 3), *heavy), -most, most).astype(kind)


def setup_inputs(seed: int = 0) -> dict:
    splits = jax.random.split(jax.random.key(seed), 19)
    return {
        "tokens": noise_with(splits[0], (TOKENS, D), 1.0, 6.0, ((0, 32),), (0, 1, 32, 2.75)),
        "cotangent": noise_with(splits[1], (TOKENS, D), 1.0, 6.0, ((0, 32),), (0, 1, 32, 2.75)),
        "group_size": draw_group_size(jax.random.fold_in(splits[18], 71), 0),
        "prefix_len": draw_prefix_len(jax.random.fold_in(splits[18], 71), 0),
        "sol_len": draw_sol_len(jax.random.fold_in(splits[18], 71), 0),
        "ln1_gain": jnp.clip(1.0 + 0.18 * jax.random.normal(splits[5], (D,), jnp.float32), 0.099609375, 1.8984375).astype(jnp.bfloat16),
        "ln1_bias": gaussian(splits[6], (D,), 0.5, 3.0, ((0, 32),)),
        "w_qkv": gaussian(splits[7], (D, 3 * D), D ** -0.5, 0.125, ((0, 32),)),
        "q_bias": gaussian(splits[8], (D,), 0.5, 3.0, ((0, 32),)),
        "v_bias": gaussian(splits[9], (D,), 0.5, 3.0, ((0, 32),)),
        "w_out": gaussian(splits[10], (D, D), (D // 64) ** -0.5, 1.0, ((0, 32),)),
        "out_bias": gaussian(splits[11], (D,), 0.5, 3.0, ((0, 32),)),
        "ln2_gain": jnp.clip(1.0 + 0.18 * jax.random.normal(splits[12], (D,), jnp.float32), 0.099609375, 1.8984375).astype(jnp.bfloat16),
        "ln2_bias": gaussian(splits[13], (D,), 0.5, 3.0, ((0, 32),)),
        "w_up": gaussian(splits[14], (D, FF), D ** -0.5, 0.125, ((0, 32),)),
        "up_bias": gaussian(splits[15], (FF,), 0.5, 3.0, ((0, 32),)),
        "w_down": gaussian(splits[16], (FF, D), FF ** -0.5, 0.0625, ((0, 32),)),
        "down_bias": gaussian(splits[17], (D,), 0.5, 3.0, ((0, 32),)),
    }


@jax.custom_vjp
def low(v):
    return lax.optimization_barrier(v.astype(jnp.bfloat16)).astype(jnp.float32)

@jax.custom_vjp
def low_back(v):
    return v

def low_keep(v):
    return (low(v), None)

def low_pass(kept, grad):
    return (grad,)

def back_keep(v):
    return (v, None)

def back_low(kept, grad):
    return (low(grad),)
low.defvjp(low_keep, low_pass)
low_back.defvjp(back_keep, back_low)
HIGH = lax.Precision.HIGHEST
EPSILON = 1e-05

def layer_norm(values_in, gain, shift):
    center = values_in - lax.optimization_barrier(jnp.mean(values_in, axis=-1, keepdims=True))
    spread = lax.optimization_barrier(jnp.mean(center * center, axis=-1, keepdims=True))
    return center * lax.rsqrt(spread + EPSILON) * gain + shift

def segment_of(group_count, prefix, lengths, slots):
    slot_index = jnp.arange(lengths.shape[-1], dtype=jnp.int32)
    used = lengths * (slot_index < group_count).astype(jnp.int32)
    bounds = prefix + jnp.cumsum(used).astype(jnp.int32)
    total = prefix + jnp.sum(used)
    places = jnp.arange(slots, dtype=jnp.int32)
    inside = 1 + lax.optimization_barrier(jnp.sum((bounds[None, :] <= places[:, None]).astype(jnp.int32), axis=1))
    return jnp.where(places < prefix, 0, jnp.where(places < total, inside, -1)).astype(jnp.int32)

def allowed_pairs(segment):
    places = jnp.arange(segment.shape[0], dtype=jnp.int32)
    later = places[None, :] <= places[:, None]
    same = (segment[None, :] == 0) | (segment[None, :] == segment[:, None])
    alive = segment[:, None] >= 0
    allowed = later & same & alive | (places[None, :] == places[:, None])
    return (allowed, (segment >= 0).astype(jnp.float32))

def forward_group(inputs, segment, weights):
    gain_first, shift_first, qkv_rows, query_bias, value_bias, out_rows, out_shift, gain_second, shift_second, up_rows, up_shift, down_rows, down_shift = weights
    slots, width = inputs.shape
    head_size = width // HEADS
    allowed, live_rows = allowed_pairs(segment)
    normed_first = low(layer_norm(inputs, gain_first, shift_first))
    projected = jnp.dot(normed_first, qkv_rows, precision=HIGH)
    query = low(low_back(projected[:, :width] + query_bias))
    keys = low(low_back(projected[:, width:2 * width]))
    values = low(low_back(projected[:, 2 * width:] + value_bias))
    query_heads = query.reshape(slots, HEADS, head_size)
    key_heads = keys.reshape(slots, HEADS, head_size)
    value_heads = values.reshape(slots, HEADS, head_size)
    scores = low_back(jnp.einsum('qhd,khd->hqk', query_heads, key_heads, precision=HIGH) * head_size ** (-0.5))
    scores = jnp.where(allowed[None], scores, jnp.float32(-1e+30))
    peak = lax.optimization_barrier(jnp.max(scores, axis=-1, keepdims=True))
    exponent = jnp.exp(scores - peak)
    attn_probs = low(exponent / lax.optimization_barrier(jnp.sum(exponent, axis=-1, keepdims=True)))
    context = jnp.einsum('hqk,khd->qhd', attn_probs, value_heads, precision=HIGH).reshape(slots, width)
    context = low(low_back(context * live_rows[:, None]))
    attn_branch = low_back(jnp.dot(context, out_rows, precision=HIGH) + out_shift)
    residual = inputs + attn_branch
    normed_second = low(layer_norm(residual, gain_second, shift_second))
    up_proj = low_back(jnp.dot(normed_second, up_rows, precision=HIGH) + up_shift)
    activated = low(jax.nn.gelu(up_proj, approximate=True))
    mlp_branch = low_back(jnp.dot(activated, down_rows, precision=HIGH) + down_shift)
    return residual + mlp_branch

def reference(tokens, cotangent, group_size, prefix_len, sol_len, ln1_gain, ln1_bias, w_qkv, q_bias, v_bias, w_out, out_bias, ln2_gain, ln2_bias, w_up, up_bias, w_down, down_bias):
    weights = tuple((item.astype(jnp.float32) for item in (ln1_gain, ln1_bias, w_qkv, q_bias, v_bias, w_out, out_bias, ln2_gain, ln2_bias, w_up, up_bias, w_down, down_bias)))
    slots = TOK_DEV
    width = tokens.shape[1]
    segments = jax.vmap(lambda count, prefix, lengths: segment_of(count, prefix, lengths, slots))(group_size, prefix_len, sol_len)
    per_step = 1
    while per_step * 2 <= max(1, 4096 // slots) and GROUPS % (per_step * 2) == 0:
        per_step = per_step * 2
    step_count = GROUPS // per_step
    inputs = tokens.astype(jnp.float32).reshape(step_count, per_step, slots, width)
    seg_blocks = segments.reshape(step_count, per_step, slots)

    def whole(inputs_all, *params):
        block = jax.checkpoint(lambda xblock, sblock: jax.vmap(lambda xgroup, sgroup: forward_group(xgroup, sgroup, params))(xblock, sblock))

        def advance(carry, item):
            return (carry, block(item[0], item[1]))
        _, outputs = lax.scan(advance, jnp.zeros((), jnp.float32), (inputs_all, seg_blocks))
        return outputs
    outputs, pull = jax.vjp(whole, inputs, *weights)
    grads = pull(cotangent.astype(jnp.float32).reshape(inputs.shape))
    layer_out = outputs.reshape(tokens.shape).astype(jnp.bfloat16)
    tokens_grad = grads[0].reshape(tokens.shape).astype(jnp.bfloat16)
    return (layer_out, tokens_grad, grads[1], grads[2], grads[3], grads[4], grads[5], grads[6], grads[7], grads[8], grads[9], grads[10], grads[11], grads[12], grads[13])
```

```python
import functools

import jax
import jax.numpy as jnp
from jax import lax
from jax.sharding import Mesh
from jax.sharding import PartitionSpec as P

HEADS = 16
EPSILON = 1e-05
BF = jnp.bfloat16
F32 = jnp.float32
T_AXES = ("p", "x")
R_AXES = ("h", "y", "w", "c")
ALL = ("h", "p", "y", "x", "w", "c")


def ln_parts(values_in):
    center = values_in - jnp.mean(values_in, axis=-1, keepdims=True)
    spread = jnp.mean(center * center, axis=-1, keepdims=True)
    scale = lax.rsqrt(spread + EPSILON)
    return center * scale, scale


def ln_back(d_out, gain, unit, scale):
    d_unit = d_out * gain
    mean_d = jnp.mean(d_unit, axis=-1, keepdims=True)
    mean_du = jnp.mean(d_unit * unit, axis=-1, keepdims=True)
    return (d_unit - mean_d - unit * mean_du) * scale


def segment_of(group_count, prefix, lengths, slots):
    slot_index = jnp.arange(lengths.shape[-1], dtype=jnp.int32)
    used = lengths * (slot_index < group_count).astype(jnp.int32)
    total = prefix + jnp.sum(used)
    before = (slot_index[None, :] <= slot_index[:, None]).astype(jnp.int32)
    bounds = prefix + jnp.sum(used[None, :] * before, axis=1)
    places = jnp.arange(slots, dtype=jnp.int32)
    inside = 1 + jnp.sum((bounds[None, :] <= places[:, None]).astype(jnp.int32), axis=1)
    return jnp.where(places < prefix, 0, jnp.where(places < total, inside, -1))


def gelu_tanh(inner_value):
    return jax.nn.gelu(inner_value, approximate=True)


def dot(a, b, dims):
    return lax.dot_general(a, b, (dims, ((), ())), preferred_element_type=F32)


def swap(x, axes, mask, sizes):
    count = 1
    for name in axes:
        count *= sizes[name]
    return lax.ppermute(x, axes, [(i, i ^ mask) for i in range(count)])


def gather_t(x, sizes):
    return jnp.stack([x] + [swap(x, T_AXES, m, sizes) for m in (1, 2, 3)])


def scatter_t(parts, sizes):
    total = parts[0]
    for m in (1, 2, 3):
        total = total + swap(parts[m].astype(BF), T_AXES, m, sizes).astype(F32)
    return total


def reduce_axis(x, axis, name, sizes):
    count = sizes[name]
    me = lax.axis_index(name)
    total = lax.dynamic_index_in_dim(x, me, axis, keepdims=False).astype(F32)
    for m in range(1, count):
        piece = lax.dynamic_index_in_dim(x, me ^ m, axis, keepdims=False).astype(BF)
        total = total + swap(piece, (name,), m, sizes).astype(F32)
    return total


def local(
    sizes,
    tokens,
    cotangent,
    group_size,
    prefix_len,
    sol_len,
    ln1_gain,
    ln1_bias,
    w_qkv,
    q_bias,
    v_bias,
    w_out,
    out_bias,
    ln2_gain,
    ln2_bias,
    w_up,
    up_bias,
    w_down,
    down_bias,
):
    nh, np_, ny, nx, nw, nc = (sizes[a] for a in ALL)
    nt = np_ * nx
    slots, width = tokens.shape
    rows = w_qkv.shape[0]
    hidden = w_up.shape[1]
    ff_rows = w_down.shape[0]
    ff_t = hidden // nt
    head = width // HEADS
    heads_t = HEADS // nt
    cols_t = width // nt
    score_scale = head ** (-0.5)
    pi, xi = lax.axis_index("p"), lax.axis_index("x")

    def mine(v, axes):
        for axis, at in zip(axes, (pi, xi)):
            v = lax.dynamic_index_in_dim(v, at, axis, keepdims=True)
        return v

    segment = segment_of(group_size[0], prefix_len[0], sol_len[0], slots)
    unit = hidden // width
    vectors = (ln1_gain, ln1_bias, q_bias, v_bias, out_bias, ln2_gain, ln2_bias, down_bias, up_bias)
    small = jnp.concatenate(vectors + (segment.astype(BF),))
    small_all = lax.all_gather(small, ALL, axis=0)
    at = 0
    full = []
    for v in vectors:
        full.append(small_all[:, at : at + v.shape[0]].reshape(-1).astype(F32))
        at += v.shape[0]
    gain1, bias1, qb, vb, outb, gain2, bias2, downb, upb = full
    seg_own = gather_t(segment.astype(BF).reshape(1, slots), sizes).reshape(nt, slots).astype(jnp.int32)
    qb_t = mine(qb.reshape(nh, np_, ny, nx, head), (1, 3)).reshape(cols_t)
    vb_t = mine(vb.reshape(nh, np_, ny, nx, head), (1, 3)).reshape(cols_t)
    upb_t = mine(upb.reshape(nh, np_, ny, nx, nw * nc * ff_rows), (1, 3)).reshape(ff_t)

    places = jnp.arange(slots, dtype=jnp.int32)
    later = places[None, :] <= places[:, None]
    same = (seg_own[:, None, :] == 0) | (seg_own[:, None, :] == seg_own[:, :, None])
    allowed = later[None] & same & (seg_own[:, :, None] >= 0)
    allowed = allowed | (places[None, :] == places[:, None])[None]
    live = (seg_own >= 0).astype(F32)

    def to_members(w, lead, tail):
        v = w.reshape(rows, lead, nh, np_, ny, nx, tail)
        v = v.transpose(3, 5, 0, 1, 2, 4, 6).reshape(nt, rows, lead * nh * ny * tail)
        v = lax.all_to_all(v, T_AXES, 0, 0, tiled=False)
        g = lax.all_gather(v, R_AXES, axis=0)
        g = g.reshape(nh, ny, nw * nc, np_, nx, rows, lead * nh * ny * tail)
        return g.transpose(0, 3, 1, 4, 2, 5, 6).reshape(width, lead * nh * ny * tail)

    wqkv_t = to_members(w_qkv, 3, head)
    wout_t = lax.all_gather(w_out, R_AXES, axis=0).reshape(cols_t, width)
    wup_t = to_members(w_up, 1, nw * nc * ff_rows)
    wdown_t = lax.all_gather(w_down, R_AXES, axis=0).reshape(ff_t, width)

    x_all = gather_t(tokens, sizes).reshape(nt * slots, width).astype(F32)
    unit1_all, _ = ln_parts(x_all)
    n1 = (unit1_all * gain1 + bias1).astype(BF)
    proj = dot(n1, wqkv_t, ((1,), (0,)))
    q = (proj[:, :cols_t] + qb_t).astype(BF).reshape(nt, slots, heads_t, head)
    k = proj[:, cols_t : 2 * cols_t].astype(BF).reshape(nt, slots, heads_t, head)
    v = (proj[:, 2 * cols_t :] + vb_t).astype(BF).reshape(nt, slots, heads_t, head)
    scores = jnp.einsum("mqhd,mkhd->mhqk", q, k, preferred_element_type=F32) * score_scale
    scores = jnp.where(allowed[:, None], scores, F32(-1e30))
    peak = jnp.max(scores, axis=-1, keepdims=True)
    exponent = jnp.exp(scores - peak)
    probs = exponent / jnp.sum(exponent, axis=-1, keepdims=True)
    probs_low = probs.astype(BF)
    context = jnp.einsum("mhqk,mkhd->mqhd", probs_low, v, preferred_element_type=F32)
    context = (context * live[:, :, None, None]).astype(BF).reshape(nt * slots, cols_t)
    attn = scatter_t(dot(context, wout_t, ((1,), (0,))).reshape(nt, slots, width), sizes)
    inputs = tokens.astype(F32)
    residual = inputs + attn + outb

    unit2, scale2 = ln_parts(residual)
    n2 = gather_t((unit2 * gain2 + bias2).astype(BF), sizes).reshape(nt * slots, width)
    cot = gather_t(cotangent, sizes).reshape(nt * slots, width)
    up = dot(n2, wup_t, ((1,), (0,))) + upb_t
    act = gelu_tanh(up).astype(BF)
    mlp = scatter_t(dot(act, wdown_t, ((1,), (0,))).reshape(nt, slots, width), sizes)
    layer_out = (residual + mlp + downb).astype(BF)
    d_act = dot(cot, wdown_t, ((1,), (1,)))
    _, gelu_pull = jax.vjp(gelu_tanh, up)
    d_up = gelu_pull(d_act)[0].astype(BF)
    d_n2 = scatter_t(dot(d_up, wup_t, ((1,), (1,))).reshape(nt, slots, width), sizes)
    g_down = dot(act, cot, ((0,), (0,))).astype(BF)
    g_up = dot(n2, d_up, ((0,), (0,))).astype(BF)
    cot32 = cotangent.astype(F32)
    d_residual = cot32 + ln_back(d_n2, gain2, unit2, scale2)
    d_branch = d_residual.astype(BF)

    db = gather_t(d_branch, sizes).reshape(nt * slots, width)
    g_out = dot(context, db, ((0,), (0,))).astype(BF)
    d_context = dot(db, wout_t, ((1,), (1,))).reshape(nt, slots, heads_t, head)
    d_context = (d_context * live[:, :, None, None]).astype(BF)
    d_probs = jnp.einsum("mqhd,mkhd->mhqk", d_context, v, preferred_element_type=F32)
    d_v = jnp.einsum("mhqk,mqhd->mkhd", probs_low, d_context, preferred_element_type=F32)
    inner = jnp.sum(probs * d_probs, axis=-1, keepdims=True)
    d_scores = (probs * (d_probs - inner)).astype(BF)
    d_q = jnp.einsum("mhqk,mkhd->mqhd", d_scores, k, preferred_element_type=F32) * score_scale
    d_k = jnp.einsum("mhqk,mqhd->mkhd", d_scores, q, preferred_element_type=F32) * score_scale
    d_q, d_k, d_v = (u.astype(BF).reshape(nt * slots, cols_t) for u in (d_q, d_k, d_v))
    d_qkv = jnp.concatenate([d_q, d_k, d_v], axis=1)
    d_n1 = scatter_t(dot(d_qkv, wqkv_t, ((1,), (1,))).reshape(nt, slots, width), sizes)
    g_qkv = dot(n1, d_qkv, ((0,), (0,))).astype(BF)
    unit1, scale1 = ln_parts(inputs)
    tokens_grad = (d_residual + ln_back(d_n1, gain1, unit1, scale1)).astype(BF)

    def reduce_replicas(g, axis_of):
        for name in ("c", "w", "y", "h"):
            g = reduce_axis(g, axis_of[name], name, sizes)
        return g

    def from_members(g, lead, tail):
        per = lead * nh * ny * tail
        g = g.reshape(nh, np_, ny, nx, nw, nc, rows, per)
        g = reduce_replicas(g, {"c": 5, "w": 4, "y": 2, "h": 0})
        g = lax.all_to_all(g.astype(BF).reshape(nt, rows, per), T_AXES, 0, 0, tiled=False)
        g = g.reshape(np_, nx, rows, lead, nh, ny, tail).transpose(2, 3, 4, 0, 5, 1, 6)
        return g.reshape(rows, lead * nh * np_ * ny * nx * tail).astype(F32)

    w_down_grad = reduce_replicas(
        g_down.reshape(nh, ny, nw, nc, ff_rows, width), {"c": 3, "w": 2, "y": 1, "h": 0}
    )
    w_up_grad = from_members(g_up, 1, nw * nc * ff_rows)
    w_out_grad = reduce_replicas(
        g_out.reshape(nh, ny, nw, nc, rows, width), {"c": 3, "w": 2, "y": 1, "h": 0}
    )
    w_qkv_grad = from_members(g_qkv, 3, head)

    def spread(v, tail):
        v = v.reshape(nh, 1, ny, 1, tail)
        pick = (jnp.arange(np_) == pi).astype(F32).reshape(1, np_, 1, 1, 1)
        pick = pick * (jnp.arange(nx) == xi).astype(F32).reshape(1, 1, 1, nx, 1)
        return (v * pick).reshape(-1)

    terms = (
        jnp.sum(d_n1 * unit1, axis=0),
        jnp.sum(d_n1, axis=0),
        spread(jnp.sum(d_q, axis=0, dtype=F32), head),
        spread(jnp.sum(d_v, axis=0, dtype=F32), head),
        jnp.sum(d_branch, axis=0, dtype=F32),
        jnp.sum(d_n2 * unit2, axis=0),
        jnp.sum(d_n2, axis=0),
        jnp.sum(cotangent, axis=0, dtype=F32),
        spread(jnp.sum(d_up, axis=0, dtype=F32), nw * nc * ff_rows),
    )
    count = nh * np_ * ny * nx * nw * nc
    packed = jnp.concatenate([v.reshape(count, -1) for v in terms], axis=1)
    packed = lax.psum_scatter(packed, ALL, scatter_dimension=0, tiled=True)[0]
    at = 0
    outs = []
    for v in vectors:
        outs.append(packed[at : at + v.shape[0]])
        at += v.shape[0]
    g1, b1, gq, gv, go, g2, b2, gd, gu = outs
    return (
        layer_out,
        tokens_grad,
        g1,
        b1,
        w_qkv_grad,
        gq,
        gv,
        w_out_grad,
        go,
        g2,
        b2,
        w_up_grad,
        gu,
        w_down_grad,
        gd,
    )


def solution(mesh):
    dp, fsdp = mesh.shape["dp"], mesh.shape["fsdp"]
    shape = (2, 2, 2, 2, dp // 16, fsdp)
    sizes = dict(zip(ALL, shape))
    grid = Mesh(mesh.devices.reshape(shape), ALL)
    row, flat = P(ALL, None), P(ALL)
    return jax.shard_map(
        functools.partial(local, sizes),
        mesh=grid,
        in_specs=(row, row, flat, flat, row, flat, flat, row, flat, flat, row, flat, flat, flat)
        + (row, flat, row, flat),
        out_specs=(row, row, flat, flat, row, flat, flat, row, flat, flat, flat, row, flat)
        + (row, flat),
        check_vma=False,
    )
```

```python
import functools

import jax
import jax.numpy as jnp
from jax import lax
from jax.experimental import pallas as pl
from jax.experimental.pallas import tpu as pltpu
from jax.sharding import Mesh
from jax.sharding import PartitionSpec as P

HEADS = 16
EPSILON = 1e-05
BF = jnp.bfloat16
F32 = jnp.float32
T_AXES = ("p", "x")
R_AXES = ("h", "y", "w", "c")
ALL = ("h", "p", "y", "x", "w", "c")

MESH_ID = pl.DeviceIdType.MESH


class Wire:
    def __init__(self, sizes, send, recv, local, bounce):
        self.sizes = sizes
        self.send, self.recv, self.local, self.bounce = send, recv, local, bounce
        self.at = {name: lax.axis_index(name) for name in ALL}
        self.count = 0
        self.kept = 0
        self.sent = []

    def greet(self, axes):
        barrier = pltpu.get_barrier_semaphore()
        peers = []
        if "t" in axes:
            peers += [self.member(m) for m in (1, 2, 3)]
        for name in axes:
            if name != "t":
                peers += self.others(name)
        for peer in peers:
            pl.semaphore_signal(barrier, inc=1, device_id=peer, device_id_type=MESH_ID)
        pl.semaphore_wait(barrier, len(peers))

    def member(self, m):
        peer = {}
        if m & 2:
            peer["p"] = 1 - self.at["p"]
        if m & 1:
            peer["x"] = 1 - self.at["x"]
        return peer

    def others(self, name):
        count = self.sizes[name]
        return [{name: lax.rem(self.at[name] + k, count)} for k in range(1, count)]

    def put(self, source, target, peer):
        copy = pltpu.make_async_remote_copy(
            src_ref=source,
            dst_ref=target,
            send_sem=self.send.at[self.count],
            recv_sem=self.recv.at[self.count],
            device_id=peer,
            device_id_type=MESH_ID,
        )
        self.count += 1
        copy.start()
        self.sent.append(copy)
        return copy

    def where(self, dims, free):
        return tuple(slice(None) if d in free else self.at[d] for d in dims)

    def spread(self, ref, dims, free, name, source=None, tail=()):
        place = ref.at[self.where(dims, free) + tail]
        return [
            self.put(place if source is None else source, place, peer)
            for peer in self.others(name)
        ]

    def keep(self, source, target):
        room = self.bounce[self.kept]
        sem = self.local.at[self.kept]
        self.kept += 1
        first = pltpu.make_async_copy(source, room, sem)
        first.start()
        second = pltpu.make_async_copy(room, target, sem)

        def go():
            first.wait()
            second.start()
            return second

        return go

    def close(self):
        for copy in self.sent:
            copy.wait_send()


def arrive(copies):
    for copy in copies:
        copy.wait_recv()


def comm_call(name, cid, sizes, body, ins, outs, bounce=(), scratch=(), copies=64):
    nb = len(bounce)

    def kernel(*refs):
        n_in, n_out = len(ins), len(outs)
        in_refs, out_refs = refs[:n_in], refs[n_in : n_in + n_out]
        rest = refs[n_in + n_out :]
        send, recv, local = rest[:3]
        wire = Wire(sizes, send, recv, local, rest[3 : 3 + nb])
        body(wire, in_refs, out_refs, rest[3 + nb :])
        wire.close()

    return pl.pallas_call(
        kernel,
        out_shape=outs,
        in_specs=[pl.BlockSpec(memory_space=pl.ANY)] * len(ins),
        out_specs=[pl.BlockSpec(memory_space=pl.ANY)] * len(outs),
        scratch_shapes=[
            pltpu.SemaphoreType.DMA((copies,)),
            pltpu.SemaphoreType.DMA((copies,)),
            pltpu.SemaphoreType.DMA((max(nb, 1),)),
        ]
        + [pltpu.VMEM(s, BF) for s in bounce]
        + list(scratch),
        compiler_params=pltpu.CompilerParams(
            collective_id=cid, has_side_effects=True, vmem_limit_bytes=60000 * 1024
        ),
        name=name,
    )(*ins)


MEMBER = "hpyxwc"
STRIPE = "hywc"


def gather_first(wire, ins, outs, _):
    tok, sm, wo, wqkv = ins[0], ins[1], ins[2], ins[3:]
    X, S, O, W = outs[0], outs[1], outs[2], outs[3:]
    at = wire.at
    own = wire.where(MEMBER, "")
    goes = [wire.keep(sm, S.at[own])]
    goes += [wire.keep(wqkv[i].at[at["p"], at["x"]], W[i].at[own]) for i in range(3)]
    goes += [wire.keep(wo, O.at[wire.where(STRIPE, "")])]
    goes += [wire.keep(tok, X.at[0])]
    wire.greet(("t", "h", "y", "c", "w"))
    s_in = [wire.put(sm, S.at[own], wire.member(m)) for m in (1, 2, 3)]
    w_in = []
    for i in range(3):
        part = []
        for m in (1, 2, 3):
            peer = wire.member(m)
            src = wqkv[i].at[peer.get("p", at["p"]), peer.get("x", at["x"])]
            part.append(wire.put(src, W[i].at[own], peer))
        w_in.append(part)
    o_in = wire.spread(O, STRIPE, "", "h", source=wo)
    x_in = [wire.put(tok, X.at[m], wire.member(m)) for m in (1, 2, 3)]
    held = [go() for go in goes]
    held[0].wait()
    arrive(s_in)
    s_in = wire.spread(S, MEMBER, "px", "h")
    for i in range(3):
        held[1 + i].wait()
        arrive(w_in[i])
        w_in[i] = wire.spread(W[i], MEMBER, "px", "h")
    held[4].wait()
    arrive(o_in)
    o_in = wire.spread(O, STRIPE, "h", "y")
    arrive(s_in)
    s_in = wire.spread(S, MEMBER, "hpx", "y")
    for i in range(3):
        arrive(w_in[i])
        w_in[i] = wire.spread(W[i], MEMBER, "hpx", "y")
        if i == 0:
            arrive(s_in)
            s_in = wire.spread(S, MEMBER, "hpyx", "c")
            arrive(o_in)
            o_in = wire.spread(O, STRIPE, "hy", "c")
    for i in range(3):
        arrive(w_in[i])
        w_in[i] = wire.spread(W[i], MEMBER, "hpyx", "c")
    for stream, ref, dims, free in [(s_in, S, MEMBER, "hpyxc"), (o_in, O, STRIPE, "hyc")] + [
        (w_in[i], W[i], MEMBER, "hpyxc") for i in range(3)
    ]:
        arrive(stream)
        arrive(wire.spread(ref, dims, free, "w"))
    held[5].wait()
    arrive(x_in)


def gather_second(chunks, wire, ins, outs, _):
    parts, wd, wu = ins
    R, D, U = outs
    at = wire.at
    own = wire.where(STRIPE, "")
    goes = [wire.keep(wd, D.at[own]), wire.keep(wu.at[at["p"], at["x"]], U.at[at["p"], at["x"]])]
    wire.greet(("t", "h", "y", "c", "w"))
    r_in = [wire.put(parts.at[m], R.at[m - 1], wire.member(m)) for m in (1, 2, 3)]
    rows = wd.shape[0] // chunks
    cut = [(pl.ds(i * rows, rows),) for i in range(chunks)]
    d_in = [
        wire.spread(D, STRIPE, "", "h", source=wd.at[cut[i]], tail=cut[i]) for i in range(chunks)
    ]
    u_in = []
    for m in (1, 2, 3):
        peer = wire.member(m)
        src = wu.at[peer.get("p", at["p"]), peer.get("x", at["x"])]
        u_in.append(wire.put(src, U.at[at["p"], at["x"]], peer))
    held = [go() for go in goes]
    held[0].wait()
    held[1].wait()
    for name, free in (("y", "h"), ("c", "hy"), ("w", "hyc")):
        for i in range(chunks):
            arrive(d_in[i])
            d_in[i] = wire.spread(D, STRIPE, free, name, tail=cut[i])
    for i in range(chunks):
        arrive(d_in[i])
    arrive(u_in)
    arrive(r_in)


def gather_third(chunks, wire, ins, outs, _):
    n2, cot, wu = ins
    N, C, U = outs
    own = wire.where(MEMBER, "px")
    goes = [wire.keep(wu, U.at[own]), wire.keep(n2, N.at[0]), wire.keep(cot, C.at[0])]
    wire.greet(("t", "h", "y", "c", "w"))
    n_in = [wire.put(n2, N.at[m], wire.member(m)) for m in (1, 2, 3)]
    rows = wu.shape[2] // chunks
    every = (slice(None),) * 2
    cut = [(pl.ds(i * rows, rows),) for i in range(chunks)]
    u_in = [
        wire.spread(U, MEMBER, "px", "h", source=wu.at[every + cut[i]], tail=cut[i])
        for i in range(chunks)
    ]
    n_in += [wire.put(cot, C.at[m], wire.member(m)) for m in (1, 2, 3)]
    held = [go() for go in goes]
    for h in held:
        h.wait()
    for name, free in (("y", "hpx"), ("c", "hpyx"), ("w", "hpyxc")):
        for i in range(chunks):
            arrive(u_in[i])
            u_in[i] = wire.spread(U, MEMBER, free, name, tail=cut[i])
    for i in range(chunks):
        arrive(u_in[i])
    arrive(n_in)


def shape_of(*dims):
    return jax.ShapeDtypeStruct(dims, BF)


def ln_parts(values_in):
    center = values_in - jnp.mean(values_in, axis=-1, keepdims=True)
    spread = jnp.mean(center * center, axis=-1, keepdims=True)
    scale = lax.rsqrt(spread + EPSILON)
    return center * scale, scale


def ln_back(d_out, gain, unit, scale):
    d_unit = d_out * gain
    mean_d = jnp.mean(d_unit, axis=-1, keepdims=True)
    mean_du = jnp.mean(d_unit * unit, axis=-1, keepdims=True)
    return (d_unit - mean_d - unit * mean_du) * scale


def segment_of(group_count, prefix, lengths, slots):
    slot_index = jnp.arange(lengths.shape[-1], dtype=jnp.int32)
    used = lengths * (slot_index < group_count).astype(jnp.int32)
    total = prefix + jnp.sum(used)
    before = (slot_index[None, :] <= slot_index[:, None]).astype(jnp.int32)
    bounds = prefix + jnp.sum(used[None, :] * before, axis=1)
    places = jnp.arange(slots, dtype=jnp.int32)
    inside = 1 + jnp.sum((bounds[None, :] <= places[:, None]).astype(jnp.int32), axis=1)
    return jnp.where(places < prefix, 0, jnp.where(places < total, inside, -1))


def gelu_tanh(inner_value):
    return jax.nn.gelu(inner_value, approximate=True)


def dot(a, b, dims):
    return lax.dot_general(a, b, (dims, ((), ())), preferred_element_type=F32)


def swap(x, axes, mask, sizes):
    count = 1
    for name in axes:
        count *= sizes[name]
    return lax.ppermute(x, axes, [(i, i ^ mask) for i in range(count)])


def gather_t(x, sizes):
    return jnp.stack([x] + [swap(x, T_AXES, m, sizes) for m in (1, 2, 3)])


def scatter_t(parts, sizes):
    total = parts[0]
    for m in (1, 2, 3):
        total = total + swap(parts[m].astype(BF), T_AXES, m, sizes).astype(F32)
    return total


def reduce_axis(x, axis, name, sizes):
    count = sizes[name]
    me = lax.axis_index(name)
    total = lax.dynamic_index_in_dim(x, me, axis, keepdims=False).astype(F32)
    for m in range(1, count):
        piece = lax.dynamic_index_in_dim(x, me ^ m, axis, keepdims=False).astype(BF)
        total = total + swap(piece, (name,), m, sizes).astype(F32)
    return total


def local(
    sizes,
    tokens,
    cotangent,
    group_size,
    prefix_len,
    sol_len,
    ln1_gain,
    ln1_bias,
    w_qkv,
    q_bias,
    v_bias,
    w_out,
    out_bias,
    ln2_gain,
    ln2_bias,
    w_up,
    up_bias,
    w_down,
    down_bias,
):
    nh, np_, ny, nx, nw, nc = (sizes[a] for a in ALL)
    nt = np_ * nx
    slots, width = tokens.shape
    rows = w_qkv.shape[0]
    hidden = w_up.shape[1]
    ff_rows = w_down.shape[0]
    ff_t = hidden // nt
    head = width // HEADS
    heads_t = HEADS // nt
    cols_t = width // nt
    score_scale = head ** (-0.5)
    pi, xi = lax.axis_index("p"), lax.axis_index("x")

    def mine(v, axes):
        for axis, at in zip(axes, (pi, xi)):
            v = lax.dynamic_index_in_dim(v, at, axis, keepdims=True)
        return v

    segment = segment_of(group_size[0], prefix_len[0], sol_len[0], slots)
    unit = hidden // width
    vectors = (ln1_gain, ln1_bias, q_bias, v_bias, out_bias, ln2_gain, ln2_bias, down_bias, up_bias)
    small = jnp.concatenate(vectors + (segment.astype(BF),))
    lead = (nh, np_, ny, nx, nw, nc)
    small = jnp.pad(small, (0, 1024 - small.shape[0])).reshape(8, 128)
    wq = w_qkv.reshape(rows, 3, nh, np_, ny, nx, head).transpose(1, 3, 5, 0, 2, 4, 6)
    wq = wq.reshape(3, np_, nx, rows, cols_t)
    wu = w_up.reshape(rows, nh, np_, ny, nx, nw * nc * ff_rows).transpose(2, 4, 0, 1, 3, 5)
    wu = wu.reshape(np_, nx, rows, ff_t)
    x_all, small_all, wout_t, wq_t, wk_t, wv_t = comm_call(
        "gather_first",
        1,
        sizes,
        gather_first,
        (tokens, small, w_out, wq[0], wq[1], wq[2]),
        (
            shape_of(nt, slots, width),
            shape_of(*lead, 8, 128),
            shape_of(nh, ny, nw, nc, rows, width),
        )
        + (shape_of(*lead, rows, cols_t),) * 3,
        bounce=((8, 128),) + ((rows, cols_t),) * 3 + ((rows, width), (slots, width)),
    )
    wout_t = wout_t.reshape(cols_t, width)
    wq_t, wk_t, wv_t = (u.reshape(width, cols_t) for u in (wq_t, wk_t, wv_t))
    small_own = lax.dynamic_slice(
        small_all.reshape(nh, np_, ny, nx, nw, nc, 1024),
        tuple(lax.axis_index(a) if a not in T_AXES else 0 for a in ALL) + (0,),
        (1, np_, 1, nx, 1, 1, 1024),
    ).reshape(nt, 1024)
    small_all = small_all.reshape(-1, 1024)
    at = 0
    full = []
    for v in vectors:
        full.append(small_all[:, at : at + v.shape[0]].reshape(-1).astype(F32))
        at += v.shape[0]
    gain1, bias1, qb, vb, outb, gain2, bias2, downb, upb = full
    seg_own = small_own[:, at : at + slots]
    seg_own = jnp.where(xi == 0, seg_own, seg_own.reshape(2, 2, slots)[:, ::-1].reshape(4, slots))
    seg_own = jnp.where(pi == 0, seg_own, seg_own.reshape(2, 2, slots)[::-1].reshape(4, slots))
    seg_own = seg_own.astype(jnp.int32)
    qb_t = mine(qb.reshape(nh, np_, ny, nx, head), (1, 3)).reshape(cols_t)
    vb_t = mine(vb.reshape(nh, np_, ny, nx, head), (1, 3)).reshape(cols_t)
    upb_t = mine(upb.reshape(nh, np_, ny, nx, nw * nc * ff_rows), (1, 3)).reshape(ff_t)

    places = jnp.arange(slots, dtype=jnp.int32)
    later = places[None, :] <= places[:, None]
    same = (seg_own[:, None, :] == 0) | (seg_own[:, None, :] == seg_own[:, :, None])
    allowed = later[None] & same & (seg_own[:, :, None] >= 0)
    allowed = allowed | (places[None, :] == places[:, None])[None]
    live = (seg_own >= 0).astype(F32)

    x_all = x_all.reshape(nt * slots, width).astype(F32)
    unit1_all, _ = ln_parts(x_all)
    n1 = (unit1_all * gain1 + bias1).astype(BF)
    q = (dot(n1, wq_t, ((1,), (0,))) + qb_t).astype(BF).reshape(nt, slots, heads_t, head)
    k = dot(n1, wk_t, ((1,), (0,))).astype(BF).reshape(nt, slots, heads_t, head)
    v = (dot(n1, wv_t, ((1,), (0,))) + vb_t).astype(BF).reshape(nt, slots, heads_t, head)
    scores = jnp.einsum("mqhd,mkhd->mhqk", q, k, preferred_element_type=F32) * score_scale
    scores = jnp.where(allowed[:, None], scores, F32(-1e30))
    peak = jnp.max(scores, axis=-1, keepdims=True)
    exponent = jnp.exp(scores - peak)
    probs = exponent / jnp.sum(exponent, axis=-1, keepdims=True)
    probs_low = probs.astype(BF)
    context = jnp.einsum("mhqk,mkhd->mqhd", probs_low, v, preferred_element_type=F32)
    context = (context * live[:, :, None, None]).astype(BF).reshape(nt * slots, cols_t)
    part = dot(context, wout_t, ((1,), (0,))).reshape(nt, slots, width)
    others, wdown_t, wu = comm_call(
        "gather_second",
        2,
        sizes,
        functools.partial(gather_second, 4),
        (part.astype(BF), w_down, wu),
        (
            shape_of(nt - 1, slots, width),
            shape_of(nh, ny, nw, nc, ff_rows, width),
            shape_of(np_, nx, rows, ff_t),
        ),
        bounce=((ff_rows, width), (rows, ff_t)),
    )
    wdown_t = wdown_t.reshape(ff_t, width)
    inputs = tokens.astype(F32)
    residual = inputs + part[0] + jnp.sum(others.astype(F32), axis=0) + outb

    unit2, scale2 = ln_parts(residual)
    n2, cot, wup_t = comm_call(
        "gather_third",
        3,
        sizes,
        functools.partial(gather_third, 4 if rows % 64 == 0 else 1),
        ((unit2 * gain2 + bias2).astype(BF), cotangent, wu),
        (
            shape_of(nt, slots, width),
            shape_of(nt, slots, width),
            shape_of(*lead, rows, ff_t),
        ),
        bounce=((np_, nx, rows, ff_t), (slots, width), (slots, width)),
    )
    n2, cot = n2.reshape(nt * slots, width), cot.reshape(nt * slots, width)
    wup_t = wup_t.reshape(width, ff_t)
    up = dot(n2, wup_t, ((1,), (0,))) + upb_t
    act = gelu_tanh(up).astype(BF)
    mlp = scatter_t(dot(act, wdown_t, ((1,), (0,))).reshape(nt, slots, width), sizes)
    layer_out = (residual + mlp + downb).astype(BF)
    d_act = dot(cot, wdown_t, ((1,), (1,)))
    _, gelu_pull = jax.vjp(gelu_tanh, up)
    d_up = gelu_pull(d_act)[0].astype(BF)
    d_n2 = scatter_t(dot(d_up, wup_t, ((1,), (1,))).reshape(nt, slots, width), sizes)
    g_down = dot(act, cot, ((0,), (0,))).astype(BF)
    g_up = dot(n2, d_up, ((0,), (0,))).astype(BF)
    cot32 = cotangent.astype(F32)
    d_residual = cot32 + ln_back(d_n2, gain2, unit2, scale2)
    d_branch = d_residual.astype(BF)

    db = gather_t(d_branch, sizes).reshape(nt * slots, width)
    g_out = dot(context, db, ((0,), (0,))).astype(BF)
    d_context = dot(db, wout_t, ((1,), (1,))).reshape(nt, slots, heads_t, head)
    d_context = (d_context * live[:, :, None, None]).astype(BF)
    d_probs = jnp.einsum("mqhd,mkhd->mhqk", d_context, v, preferred_element_type=F32)
    d_v = jnp.einsum("mhqk,mqhd->mkhd", probs_low, d_context, preferred_element_type=F32)
    inner = jnp.sum(probs * d_probs, axis=-1, keepdims=True)
    d_scores = (probs * (d_probs - inner)).astype(BF)
    d_q = jnp.einsum("mhqk,mkhd->mqhd", d_scores, k, preferred_element_type=F32) * score_scale
    d_k = jnp.einsum("mhqk,mqhd->mkhd", d_scores, q, preferred_element_type=F32) * score_scale
    d_q, d_k, d_v = (u.astype(BF).reshape(nt * slots, cols_t) for u in (d_q, d_k, d_v))
    d_qkv = jnp.concatenate([d_q, d_k, d_v], axis=1)
    d_n1 = dot(d_q, wq_t, ((1,), (1,))) + dot(d_k, wk_t, ((1,), (1,))) + dot(d_v, wv_t, ((1,), (1,)))
    d_n1 = scatter_t(d_n1.reshape(nt, slots, width), sizes)
    g_qkv = dot(n1, d_qkv, ((0,), (0,))).astype(BF)
    unit1, scale1 = ln_parts(inputs)
    tokens_grad = (d_residual + ln_back(d_n1, gain1, unit1, scale1)).astype(BF)

    def reduce_replicas(g, axis_of):
        for name in ("c", "w", "y", "h"):
            g = reduce_axis(g, axis_of[name], name, sizes)
        return g

    def from_members(g, lead, tail):
        per = lead * nh * ny * tail
        g = g.reshape(nh, np_, ny, nx, nw, nc, rows, per)
        g = reduce_replicas(g, {"c": 5, "w": 4, "y": 2, "h": 0})
        g = lax.all_to_all(g.astype(BF).reshape(nt, rows, per), T_AXES, 0, 0, tiled=False)
        g = g.reshape(np_, nx, rows, lead, nh, ny, tail).transpose(2, 3, 4, 0, 5, 1, 6)
        return g.reshape(rows, lead * nh * np_ * ny * nx * tail).astype(F32)

    w_down_grad = reduce_replicas(
        g_down.reshape(nh, ny, nw, nc, ff_rows, width), {"c": 3, "w": 2, "y": 1, "h": 0}
    )
    w_up_grad = from_members(g_up, 1, nw * nc * ff_rows)
    w_out_grad = reduce_replicas(
        g_out.reshape(nh, ny, nw, nc, rows, width), {"c": 3, "w": 2, "y": 1, "h": 0}
    )
    w_qkv_grad = from_members(g_qkv, 3, head)

    def spread(v, tail):
        v = v.reshape(nh, 1, ny, 1, tail)
        pick = (jnp.arange(np_) == pi).astype(F32).reshape(1, np_, 1, 1, 1)
        pick = pick * (jnp.arange(nx) == xi).astype(F32).reshape(1, 1, 1, nx, 1)
        return (v * pick).reshape(-1)

    terms = (
        jnp.sum(d_n1 * unit1, axis=0),
        jnp.sum(d_n1, axis=0),
        spread(jnp.sum(d_q, axis=0, dtype=F32), head),
        spread(jnp.sum(d_v, axis=0, dtype=F32), head),
        jnp.sum(d_branch, axis=0, dtype=F32),
        jnp.sum(d_n2 * unit2, axis=0),
        jnp.sum(d_n2, axis=0),
        jnp.sum(cotangent, axis=0, dtype=F32),
        spread(jnp.sum(d_up, axis=0, dtype=F32), nw * nc * ff_rows),
    )
    count = nh * np_ * ny * nx * nw * nc
    packed = jnp.concatenate([v.reshape(count, -1) for v in terms], axis=1)
    packed = lax.psum_scatter(packed, ALL, scatter_dimension=0, tiled=True)[0]
    at = 0
    outs = []
    for v in vectors:
        outs.append(packed[at : at + v.shape[0]])
        at += v.shape[0]
    g1, b1, gq, gv, go, g2, b2, gd, gu = outs
    return (
        layer_out,
        tokens_grad,
        g1,
        b1,
        w_qkv_grad,
        gq,
        gv,
        w_out_grad,
        go,
        g2,
        b2,
        w_up_grad,
        gu,
        w_down_grad,
        gd,
    )


def solution(mesh):
    dp, fsdp = mesh.shape["dp"], mesh.shape["fsdp"]
    shape = (2, 2, 2, 2, dp // 16, fsdp)
    sizes = dict(zip(ALL, shape))
    grid = Mesh(mesh.devices.reshape(shape), ALL)
    row, flat = P(ALL, None), P(ALL)
    return jax.shard_map(
        functools.partial(local, sizes),
        mesh=grid,
        in_specs=(row, row, flat, flat, row, flat, flat, row, flat, flat, row, flat, flat, flat)
        + (row, flat, row, flat),
        out_specs=(row, row, flat, flat, row, flat, flat, row, flat, flat, flat, row, flat)
        + (row, flat),
        check_vma=False,
    )
```
